128 devices in a mesh: band: 8 (over z, core), row: 16 (over x, y).
Axes of the slice: x: 4, y: 4, z: 4, core: 2. Of those that a mesh axis runs over, the one named last changes fastest.
Arguments:
- recorded: bfloat16 [1024, 1024, 512], P(('row', 'band')), may hold values from -5 to 5
- acquired: int32 [128, 128], replicated, may hold values 0 or 1
- partner: int32 [128], replicated, may hold values from 0 to 127, each once
- band_counts: int32 [8], replicated, may hold values from 1 to 6, 32 in all
- wavelet: float32 [2, 8], replicated, may hold values from -0.75 to 0.75, as said below
Outputs:
- primaries: bfloat16 [1024, 1024, 512], P(('row', 'band'))
The draws below stay inside these ranges and needn't reach their ends.
Inputs may be any that keep to these rules, and one draw needn't show every extreme that they name: `partner`: a permutation of the 128 block indices. `band_counts`: the counts sum to 32; the largest is exactly 6. `wavelet`: each column, read as a complex number, has magnitude between 0.55 and 0.75.
All inputs are finite; a program needn't handle non-finite values.
Results may differ from the reference program's by a relative error of at most 0.0085.
Values may be sent and summed in bfloat16 or wider, within the bound.
No kernel may reach another device: no remote copies, remote signals or barrier semaphores. Data moves between devices by JAX's collectives and lax.ppermute only.
A program may use at most 128 MiB of HBM per device.

```python
import math
import jax
import jax.numpy as jnp
import numpy as np
from jax import lax

NS = 1024
NT = 512
NF = 32
FLO = 4
BS = 8
ITERS = 5
NB = 128
NGROUPS = 8
CAP = 6


def draw_recorded(key, part):
    normal_part = jax.random.normal(key, (NS, NS, NT), jnp.float32)
    return jnp.clip(normal_part, -5.0, 5.0).astype(jnp.bfloat16)


def draw_wavelet(key, part):
    first_key, second_key = jax.random.split(jax.random.fold_in(key, 17))
    magnitude = jax.random.uniform(first_key, (NGROUPS,), jnp.float32, 0.55, 0.75)
    turning = jax.random.uniform(second_key, (NGROUPS,), jnp.float32, -math.pi, math.pi)
    return jnp.stack([magnitude * jnp.cos(turning), magnitude * jnp.sin(turning)], axis=0)


def touch_ends(entries, own_key, smallest, top_value):
    extent = entries.shape
    index_at = [jax.random.randint(jax.random.fold_in(own_key, axis), (), 0, extent[axis]) for axis in range(len(extent))]
    entries = entries.at[tuple(index_at)].set(smallest)
    longest = extent.index(max(extent))
    index_at[longest] = (index_at[longest] + 1) % extent[longest]
    return entries.at[tuple(index_at)].set(top_value)


def profile(number_of, total, most, skew):
    weights = [(1 << 20) // math.isqrt(standing ** skew) + 1 for standing in range(2, number_of + 1)]
    rest, counts = total - most - (number_of - 1), [1] * (number_of - 1)
    while rest > 0:
        movable = [i for i in range(number_of - 1) if counts[i] < most]
        mass, left = sum([weights[i] for i in movable]), rest
        for i in movable:
            extra = min(most - counts[i], max(1, left * weights[i] // mass), rest)
            counts[i] = counts[i] + extra
            rest = rest - extra
    return np.array([most] + counts)


def ragged(key, count, total, most, skew):
    if count == 2:
        one = jax.random.randint(key, (), max(1, total - most), min(most, total - 1) + 1)
        return jnp.stack([one, total - one])
    sizes = jnp.asarray(profile(count, total, most, skew), jnp.int32)
    twos = (count - 1) // 2
    source_of, sink = sizes[1:1 + 2 * twos:2], sizes[2:2 + 2 * twos:2]
    room = jnp.minimum(source_of - 1, most - sink)
    moved = jax.random.randint(jax.random.fold_in(key, 1), (twos,), 0, 1 << 20) % (room + 1)
    sizes = sizes.at[1:1 + 2 * twos:2].set(source_of - moved).at[2:2 + 2 * twos:2].set(sink + moved)
    return sizes[jax.random.permutation(jax.random.fold_in(key, 2), count)]


def setup_inputs(seed: int = 0) -> dict:
    arg_keys = jax.random.split(jax.random.key(seed), 6)
    return {
        "recorded": draw_recorded(jax.random.fold_in(arg_keys[5], 71), 0),
        "acquired": touch_ends((jax.random.randint(arg_keys[1], (NB, NB), 0, 4) < 3).astype(jnp.int32), jax.random.fold_in(arg_keys[1], 1), 0, 1),
        "partner": jax.random.permutation(arg_keys[2], NB).astype(jnp.int32),
        "band_counts": ragged(arg_keys[3], NGROUPS, NF, CAP, 2).astype(jnp.int32),
        "wavelet": draw_wavelet(jax.random.fold_in(arg_keys[5], 71), 0),
    }


def dft_tables():
    sample_index = jnp.arange(NT, dtype=jnp.int32)
    bin_index = FLO + jnp.arange(NF, dtype=jnp.int32)
    angles = (bin_index[:, None] * sample_index[None, :] % NT).astype(jnp.float32) * (2.0 * math.pi / NT)
    cycles = jnp.concatenate([jnp.cos(angles), -jnp.sin(angles)], axis=0)
    forward = (cycles * (1.0 / math.sqrt(NT))).astype(jnp.bfloat16)
    inverse = (cycles * math.sqrt(2.0 / NF)).astype(jnp.bfloat16)
    return (forward, inverse)

def reference(recorded, acquired, partner, band_counts, wavelet):
    forward, inverse = dft_tables()
    block_rows = min(32, NS)
    block_total = NS // block_rows
    forward_wide = forward.astype(jnp.float32)
    inverse_wide = inverse.astype(jnp.float32)

    def transform(shot_block):
        return jnp.einsum('ct,srt->csr', forward_wide, shot_block.astype(jnp.float32), precision=lax.Precision.HIGHEST).astype(jnp.bfloat16)
    spectra = lax.map(transform, recorded.reshape(block_total, block_rows, NS, NT))
    spectra = jnp.moveaxis(spectra, 1, 0).reshape(2 * NF, NS, NS)
    offsets = jnp.arange(BS, dtype=jnp.int32)
    mirror_index = (BS * partner[:, None] + offsets[None, :]).reshape(NS).astype(jnp.int32)
    present = jnp.repeat(jnp.repeat(acquired, BS, axis=0), BS, axis=1) == 1
    mirrored = jnp.take(jnp.take(spectra, mirror_index, axis=1), mirror_index, axis=2)
    filled = jnp.where(present[None], spectra, jnp.swapaxes(mirrored, 1, 2))
    band_ends = jnp.cumsum(band_counts).astype(jnp.int32)
    bin_index = jnp.arange(NF, dtype=jnp.int32)
    bin_group = lax.optimization_barrier(jnp.sum((band_ends[None, :] <= bin_index[:, None]).astype(jnp.int32), axis=1))
    rescale = 1.0 / math.sqrt(NS)
    wave_re = wavelet[0][bin_group] * rescale
    wave_im = wavelet[1][bin_group] * rescale

    def solve(items):
        data_re, data_im, scale_re, scale_im = items
        base_re = data_re.astype(jnp.float32)
        base_im = data_im.astype(jnp.float32)
        factor_re = (scale_re * base_re - scale_im * base_im).astype(jnp.bfloat16)
        factor_im = (scale_re * base_im + scale_im * base_re).astype(jnp.bfloat16)
        factor_re, factor_im = lax.optimization_barrier((factor_re, factor_im))
        wide_fre = factor_re.astype(jnp.float32)
        wide_fim = factor_im.astype(jnp.float32)
        left_re, left_im = (data_re, data_im)
        for sweep_turn in range(ITERS):
            wide_lre = left_re.astype(jnp.float32)
            wide_lim = left_im.astype(jnp.float32)
            real_part = jnp.dot(wide_lre, wide_fre, precision=lax.Precision.HIGHEST) - jnp.dot(wide_lim, wide_fim, precision=lax.Precision.HIGHEST)
            imag_part = jnp.dot(wide_lre, wide_fim, precision=lax.Precision.HIGHEST) + jnp.dot(wide_lim, wide_fre, precision=lax.Precision.HIGHEST)
            left_re = (base_re - real_part).astype(jnp.bfloat16)
            left_im = (base_im - imag_part).astype(jnp.bfloat16)
            left_re, left_im = lax.optimization_barrier((left_re, left_im))
        return (left_re, left_im)
    estimate_re, estimate_im = lax.map(solve, (filled[:NF], filled[NF:], wave_re, wave_im))
    estimate = jnp.concatenate([estimate_re, estimate_im], axis=0)
    shot_blocks = jnp.moveaxis(estimate.reshape(2 * NF, block_total, block_rows, NS), 1, 0)

    def restore(shot_block):
        return jnp.einsum('csr,ct->srt', shot_block.astype(jnp.float32), inverse_wide, precision=lax.Precision.HIGHEST).astype(jnp.bfloat16)
    return lax.map(restore, shot_blocks).reshape(NS, NS, NT)
```

```python
import math

import jax
import jax.numpy as jnp
import ml_dtypes
import numpy as np
from jax import lax
from jax.experimental import pallas as pl
from jax.experimental.pallas import tpu as pltpu
from jax.sharding import Mesh
from jax.sharding import PartitionSpec as P

NS = 1024
NT = 512
NF = 32
FLO = 4
BS = 8
ITERS = 5
NB = NS // BS
GROUP = 32
OWN = GROUP * BS
ALL_AXES = ("z_hi", "z_lo", "core", "x", "y")
BIN_AXES = ("z_lo", "x", "y")
SHOT_AXES = ("x", "y", "z_hi", "z_lo", "core")


def dft_tables():
    sample_index = np.arange(NT, dtype=np.int32)
    bin_index = FLO + np.arange(NF, dtype=np.int32)
    angles = (bin_index[:, None] * sample_index[None, :] % NT).astype(np.float32) * np.float32(
        2.0 * math.pi / NT
    )
    cycles = np.concatenate([np.cos(angles), -np.sin(angles)], axis=0).astype(np.float32)
    forward = (cycles * np.float32(1.0 / math.sqrt(NT))).astype(ml_dtypes.bfloat16)
    inverse = (cycles * np.float32(math.sqrt(2.0 / NF))).astype(ml_dtypes.bfloat16)
    return (forward, inverse)


def source_of(block):
    return (block % 8) * 16 + block // 8


def solve_kernel(
    partner, place, wave, acquired, first, second, out, mirror, factor, left, base, mask
):
    parts = (first, second)
    column_block = lax.broadcasted_iota(jnp.int32, (NB, NS), 1) // BS
    expand = (column_block == lax.broadcasted_iota(jnp.int32, (NB, NS), 0)).astype(jnp.bfloat16)
    mask[...] = jnp.dot(
        acquired[...].astype(jnp.float32).astype(jnp.bfloat16),
        expand,
        preferred_element_type=jnp.float32,
    )

    def turn(group, carry):
        blocks = [partner[group * 16 + i] for i in range(16)]
        for part in range(2):
            rows = jnp.concatenate(
                [parts[part][source_of(block)].astype(jnp.float32) for block in blocks], axis=0
            )
            mirror[part, :, pl.ds(pl.multiple_of(group * 128, 128), 128)] = rows.T
        return carry

    lax.fori_loop(0, NB // 16, turn, 0)

    def filled(block):
        keep = mask[pl.ds(block, 1), :] > 0.5
        row = pl.multiple_of(partner[block] * BS, BS)
        source = source_of(block)
        return tuple(
            jnp.where(
                keep, parts[part][source].astype(jnp.float32), mirror[part, pl.ds(row, BS), :]
            )
            for part in range(2)
        )

    def scale(pair, carry):
        upper = filled(pair * 2)
        lower = filled(pair * 2 + 1)
        real = jnp.concatenate([upper[0], lower[0]], axis=0)
        imag = jnp.concatenate([upper[1], lower[1]], axis=0)
        row = pl.multiple_of(pair * 16, 16)
        factor[pl.ds(row, 16), :] = (wave[0] * real - wave[1] * imag).astype(jnp.bfloat16)
        factor[pl.ds(NS + row, 16), :] = (wave[0] * imag + wave[1] * real).astype(jnp.bfloat16)
        return carry

    lax.fori_loop(0, NB // 2, scale, 0)

    def put(slot, row, rows, real, imag, column, columns):
        real_low = real.astype(jnp.bfloat16)
        imag_low = imag.astype(jnp.bfloat16)
        left[slot, pl.ds(row, rows), pl.ds(column, columns)] = real_low
        left[slot, pl.ds(row, rows), pl.ds(NS + column, columns)] = -imag_low
        left[slot, pl.ds(OWN + row, rows), pl.ds(column, columns)] = imag_low
        left[slot, pl.ds(OWN + row, rows), pl.ds(NS + column, columns)] = real_low

    def own(pair, carry):
        blocks = []
        for i in range(2):
            member = pair * 2 + i
            blocks.append(filled((member % 16) * 8 + (member // 16) * 2 + place[0]))
        real = jnp.concatenate([blocks[0][0], blocks[1][0]], axis=0)
        imag = jnp.concatenate([blocks[0][1], blocks[1][1]], axis=0)
        row = pl.multiple_of(pair * 16, 16)
        base[pl.ds(row, 16), :] = real
        base[pl.ds(OWN + row, 16), :] = imag
        put(0, row, 16, real, imag, 0, NS)
        return carry

    lax.fori_loop(0, GROUP // 2, own, 0)

    width = 256

    def sweep(slot, last):
        for tile in range(NS // width):
            columns = pl.ds(tile * width, width)
            product = jnp.dot(
                left[slot], factor[:, columns], preferred_element_type=jnp.float32
            )
            value = base[:, columns] - product
            if last:
                out[:, 0, :, columns] = (
                    value[:OWN].reshape(GROUP, BS, width).astype(jnp.bfloat16)
                )
                out[:, 1, :, columns] = (
                    value[OWN:].reshape(GROUP, BS, width).astype(jnp.bfloat16)
                )
            else:
                put(1 - slot, 0, OWN, value[:OWN], value[OWN:], tile * width, width)

    for turn_index in range(ITERS):
        sweep(turn_index % 2, turn_index == ITERS - 1)


def solve(partner, place, wave, acquired, first, second):
    smem = pl.BlockSpec(memory_space=pltpu.SMEM)
    vmem = pl.BlockSpec(memory_space=pltpu.VMEM)
    return pl.pallas_call(
        solve_kernel,
        out_shape=jax.ShapeDtypeStruct((GROUP, 2, BS, NS), jnp.bfloat16),
        in_specs=[smem, smem, smem, vmem, vmem, vmem],
        out_specs=vmem,
        scratch_shapes=[
            pltpu.VMEM((2, NS, NS), jnp.float32),
            pltpu.VMEM((2 * NS, NS), jnp.bfloat16),
            pltpu.VMEM((2, 2 * OWN, 2 * NS), jnp.bfloat16),
            pltpu.VMEM((2 * OWN, NS), jnp.float32),
            pltpu.VMEM((NB, NS), jnp.float32),
        ],
        compiler_params=pltpu.CompilerParams(vmem_limit_bytes=48 * 1024 * 1024),
        name="solve",
    )(partner, place, wave, acquired, first, second)


def shards(recorded, acquired, partner, band_counts, wavelet):
    core = lax.axis_index("core")
    z_hi = lax.axis_index("z_hi")
    my_bin = lax.axis_index("z_lo") * 16 + lax.axis_index("x") * 4 + lax.axis_index("y")
    forward, inverse = dft_tables()
    ordered = np.tile(forward.reshape(2, 2, 16, NT).transpose(1, 0, 2, 3).reshape(64, NT), (2, 1))
    outgoing = jnp.einsum(
        "ct,srt->csr", jnp.asarray(ordered), recorded, preferred_element_type=jnp.float32
    ).astype(jnp.bfloat16)
    first = lax.all_to_all(outgoing, ALL_AXES, split_axis=0, concat_axis=0, tiled=True)
    second = lax.ppermute(first, "core", [(0, 1), (1, 0)])

    band_ends = jnp.cumsum(band_counts)
    my_group = jnp.sum((band_ends <= my_bin).astype(jnp.int32))
    chosen = (jnp.arange(8, dtype=jnp.int32) == my_group).astype(jnp.float32)
    rescale = 1.0 / math.sqrt(NS)
    wave = jnp.sum(wavelet * chosen[None, :], axis=1) * rescale
    wave = jnp.where(core == 0, wave, -wave[::-1])
    place = (z_hi * 4 + core).astype(jnp.int32).reshape(1)
    estimate = solve(partner, place, wave, acquired, first, second)

    returned = lax.all_to_all(estimate, BIN_AXES, split_axis=0, concat_axis=0, tiled=True)
    table = inverse.reshape(2, NF, NT)
    table = jnp.where(core == 0, jnp.asarray(table), jnp.asarray(table[::-1]))
    output = jnp.einsum("kcsr,ckt->srt", returned, table, preferred_element_type=jnp.float32)
    return output.astype(jnp.bfloat16)


def solution(mesh):
    fine = Mesh(mesh.devices.reshape(2, 2, 2, 4, 4), ALL_AXES)
    return jax.shard_map(
        shards,
        mesh=fine,
        in_specs=(P(SHOT_AXES, None, None), P(), P(), P(), P()),
        out_specs=P(SHOT_AXES, None, None),
        check_vma=False,
    )
```

```python
import math

import jax
import jax.numpy as jnp
import ml_dtypes
import numpy as np
from jax import lax
from jax.experimental import pallas as pl
from jax.experimental.pallas import tpu as pltpu
from jax.sharding import Mesh
from jax.sharding import PartitionSpec as P

NS = 1024
NT = 512
NF = 32
FLO = 4
BS = 8
ITERS = 5
NB = NS // BS
GROUP = 32
OWN = GROUP * BS
ALL_AXES = ("z_hi", "z_lo", "core", "x", "y")
BIN_AXES = ("z_lo", "x", "y")
SHOT_AXES = ("x", "y", "z_hi", "z_lo", "core")


def dft_tables():
    sample_index = np.arange(NT, dtype=np.int32)
    bin_index = FLO + np.arange(NF, dtype=np.int32)
    angles = (bin_index[:, None] * sample_index[None, :] % NT).astype(np.float32) * np.float32(
        2.0 * math.pi / NT
    )
    cycles = np.concatenate([np.cos(angles), -np.sin(angles)], axis=0).astype(np.float32)
    forward = (cycles * np.float32(1.0 / math.sqrt(NT))).astype(ml_dtypes.bfloat16)
    inverse = (cycles * np.float32(math.sqrt(2.0 / NF))).astype(ml_dtypes.bfloat16)
    return (forward, inverse)


def source_of(block):
    return (block % 8) * 16 + block // 8


def transform_kernel(table_from, traces, out, table, held, wide, sems):
    shots = traces.shape[0]
    copies = [pltpu.make_async_copy(traces.at[s], held.at[s], sems.at[s]) for s in range(shots)]
    table_copy = pltpu.make_async_copy(table_from, table, sems.at[shots])
    table_copy.start()
    for copy in copies:
        copy.start()
    table_copy.wait()
    for s in range(shots):
        copies[s].wait()
        wide[s] = lax.dot_general(
            table[...], held[s], (((1,), (1,)), ((), ())), preferred_element_type=jnp.float32
        )
    ordered = jnp.transpose(wide[...], (1, 0, 2)).astype(jnp.bfloat16)
    out[:64] = ordered
    out[64:] = ordered


def transform(table, traces):
    vmem = pl.BlockSpec(memory_space=pltpu.VMEM)
    return pl.pallas_call(
        transform_kernel,
        out_shape=jax.ShapeDtypeStruct((NB, BS, NS), jnp.bfloat16),
        in_specs=[pl.BlockSpec(memory_space=pltpu.HBM)] * 2,
        out_specs=vmem,
        scratch_shapes=[
            pltpu.VMEM((2 * NF, NT), jnp.bfloat16),
            pltpu.VMEM((BS, NS, NT), jnp.bfloat16),
            pltpu.VMEM((BS, 2 * NF, NS), jnp.float32),
            pltpu.SemaphoreType.DMA((BS + 1,)),
        ],
        compiler_params=pltpu.CompilerParams(vmem_limit_bytes=24 * 1024 * 1024),
        name="transform",
    )(table, traces)


def restore_kernel(place, spectra, tables, out, wide, held, sems):
    wide[...] = jnp.transpose(
        spectra[...].astype(jnp.float32).reshape(2 * NF, BS, NS), (1, 0, 2)
    )
    table = tables[place[1]]
    copies = []
    for s in range(BS):
        held[s] = lax.dot_general(
            wide[s].astype(jnp.bfloat16),
            table,
            (((0,), (0,)), ((), ())),
            preferred_element_type=jnp.float32,
        ).astype(jnp.bfloat16)
        copies.append(pltpu.make_async_copy(held.at[s], out.at[s], sems.at[s]))
        copies[-1].start()
    for copy in copies:
        copy.wait()


def restore(place, spectra, tables):
    vmem = pl.BlockSpec(memory_space=pltpu.VMEM)
    return pl.pallas_call(
        restore_kernel,
        out_shape=jax.ShapeDtypeStruct((BS, NS, NT), jnp.bfloat16),
        in_specs=[pl.BlockSpec(memory_space=pltpu.SMEM), vmem, vmem],
        out_specs=pl.BlockSpec(memory_space=pltpu.HBM),
        scratch_shapes=[
            pltpu.VMEM((BS, 2 * NF, NS), jnp.float32),
            pltpu.VMEM((BS, NS, NT), jnp.bfloat16),
            pltpu.SemaphoreType.DMA((BS,)),
        ],
        compiler_params=pltpu.CompilerParams(vmem_limit_bytes=24 * 1024 * 1024),
        name="restore",
    )(place, spectra, tables)


def fill(partner, acquired, rows, mirror, mask, filled):
    column_block = lax.broadcasted_iota(jnp.int32, (NB, NS), 1) // BS
    expand = (column_block == lax.broadcasted_iota(jnp.int32, (NB, NS), 0)).astype(jnp.bfloat16)
    mask[...] = jnp.dot(
        acquired[...].astype(jnp.float32).astype(jnp.bfloat16),
        expand,
        preferred_element_type=jnp.float32,
    )
    size = 256
    identity = (
        lax.broadcasted_iota(jnp.int32, (size, size), 0)
        == lax.broadcasted_iota(jnp.int32, (size, size), 1)
    ).astype(jnp.bfloat16)
    for group in range(NS // size):
        taken = jnp.concatenate(
            [
                rows[source_of(partner[group * (size // BS) + i])].astype(jnp.float32)
                for i in range(size // BS)
            ],
            axis=0,
        ).astype(jnp.bfloat16)
        for tile in range(NS // size):
            turned = lax.dot_general(
                identity,
                taken[:, tile * size : (tile + 1) * size],
                (((1,), (1,)), ((), ())),
                preferred_element_type=jnp.float32,
            )
            mirror[
                tile * (size // BS) : (tile + 1) * (size // BS),
                :,
                group * size : (group + 1) * size,
            ] = turned.reshape(size // BS, BS, size).astype(jnp.bfloat16)

    def choose(pair, carry):
        blocks = []
        for i in range(2):
            block = pair * 2 + i
            keep = mask[pl.ds(block, 1), :] > 0.5
            blocks.append(
                jnp.where(
                    keep,
                    rows[source_of(block)].astype(jnp.float32),
                    mirror[partner[block]].astype(jnp.float32),
                )
            )
        row = pl.multiple_of(pair * 16, 16)
        filled[pl.ds(row, 16), :] = jnp.concatenate(blocks, axis=0).astype(jnp.bfloat16)
        return carry

    lax.fori_loop(0, NB // 2, choose, 0, unroll=8)


def fill_first_kernel(partner, acquired, rows, filled, mirror, mask):
    fill(partner, acquired, rows, mirror, mask, filled)


def fill_first(partner, acquired, rows):
    vmem = pl.BlockSpec(memory_space=pltpu.VMEM)
    return pl.pallas_call(
        fill_first_kernel,
        out_shape=jax.ShapeDtypeStruct((NS, NS), jnp.bfloat16),
        in_specs=[pl.BlockSpec(memory_space=pltpu.SMEM), vmem, vmem],
        out_specs=vmem,
        scratch_shapes=[
            pltpu.VMEM((NB, BS, NS), jnp.bfloat16),
            pltpu.VMEM((NB, NS), jnp.float32),
        ],
        compiler_params=pltpu.CompilerParams(vmem_limit_bytes=16 * 1024 * 1024),
        name="fill_first",
    )(partner, acquired, rows)


def solve_kernel(
    partner, place, wave, acquired, first, rows, out, mirror, second, factor, left, base, mask
):
    fill(partner, acquired, rows, mirror, mask, second)

    def scale(pair, carry):
        row = pl.multiple_of(pair * 16, 16)
        real = first[pl.ds(row, 16), :].astype(jnp.float32)
        imag = second[pl.ds(row, 16), :].astype(jnp.float32)
        factor[pl.ds(row, 16), :] = (wave[0] * real - wave[1] * imag).astype(jnp.bfloat16)
        factor[pl.ds(NS + row, 16), :] = (wave[0] * imag + wave[1] * real).astype(jnp.bfloat16)
        return carry

    lax.fori_loop(0, NB // 2, scale, 0, unroll=8)

    def put(slot, row, rows, real, imag, column, columns):
        real_low = real.astype(jnp.bfloat16)
        imag_low = imag.astype(jnp.bfloat16)
        left[slot, pl.ds(row, rows), pl.ds(column, columns)] = real_low
        left[slot, pl.ds(row, rows), pl.ds(NS + column, columns)] = -imag_low
        left[slot, pl.ds(OWN + row, rows), pl.ds(column, columns)] = imag_low
        left[slot, pl.ds(OWN + row, rows), pl.ds(NS + column, columns)] = real_low

    def own(pair, carry):
        values = []
        for part in (first, second):
            blocks = []
            for i in range(2):
                member = pair * 2 + i
                chip = (member % 16) * 4 + member // 16 + place[0]
                both = part[pl.ds(pl.multiple_of(chip * 16, 16), 16), :].astype(jnp.float32)
                blocks.append(jnp.where(place[1] == 0, both[:BS], both[BS:]))
            values.append(jnp.concatenate(blocks, axis=0))
        row = pl.multiple_of(pair * 16, 16)
        base[pl.ds(row, 16), :] = values[0]
        base[pl.ds(OWN + row, 16), :] = values[1]
        put(0, row, 16, values[0], values[1], 0, NS)
        return carry

    lax.fori_loop(0, GROUP // 2, own, 0, unroll=4)

    width = 256

    def sweep(slot, last):
        for tile in range(NS // width):
            columns = pl.ds(tile * width, width)
            product = jnp.dot(
                left[slot], factor[:, columns], preferred_element_type=jnp.float32
            )
            value = base[:, columns] - product
            if last:
                out[:, 0, :, columns] = (
                    value[:OWN].reshape(GROUP, BS, width).astype(jnp.bfloat16)
                )
                out[:, 1, :, columns] = (
                    value[OWN:].reshape(GROUP, BS, width).astype(jnp.bfloat16)
                )
            else:
                put(1 - slot, 0, OWN, value[:OWN], value[OWN:], tile * width, width)

    for turn_index in range(ITERS):
        sweep(turn_index % 2, turn_index == ITERS - 1)


def solve(partner, place, wave, acquired, first, rows):
    smem = pl.BlockSpec(memory_space=pltpu.SMEM)
    vmem = pl.BlockSpec(memory_space=pltpu.VMEM)
    return pl.pallas_call(
        solve_kernel,
        out_shape=jax.ShapeDtypeStruct((GROUP, 2, BS, NS), jnp.bfloat16),
        in_specs=[smem, smem, smem, vmem, vmem, vmem],
        out_specs=vmem,
        scratch_shapes=[
            pltpu.VMEM((NB, BS, NS), jnp.bfloat16),
            pltpu.VMEM((NS, NS), jnp.bfloat16),
            pltpu.VMEM((2 * NS, NS), jnp.bfloat16),
            pltpu.VMEM((2, 2 * OWN, 2 * NS), jnp.bfloat16),
            pltpu.VMEM((2 * OWN, NS), jnp.float32),
            pltpu.VMEM((NB, NS), jnp.float32),
        ],
        compiler_params=pltpu.CompilerParams(vmem_limit_bytes=32 * 1024 * 1024),
        name="solve",
    )(partner, place, wave, acquired, first, rows)


def shards(recorded, acquired, partner, band_counts, wavelet):
    core = lax.axis_index("core")
    z_hi = lax.axis_index("z_hi")
    my_bin = lax.axis_index("z_lo") * 16 + lax.axis_index("x") * 4 + lax.axis_index("y")
    place = jnp.stack([z_hi * 2, core]).astype(jnp.int32)
    forward, inverse = dft_tables()
    ordered = forward.reshape(2, 2, 16, NT).transpose(1, 0, 2, 3).reshape(2 * NF, NT)
    outgoing = transform(jnp.asarray(ordered), recorded)
    first = lax.all_to_all(outgoing, ALL_AXES, split_axis=0, concat_axis=0, tiled=True)
    second = lax.ppermute(first, "core", [(0, 1), (1, 0)])
    filled = fill_first(partner, acquired, first)

    band_ends = jnp.cumsum(band_counts)
    my_group = jnp.sum((band_ends <= my_bin).astype(jnp.int32))
    chosen = (jnp.arange(8, dtype=jnp.int32) == my_group).astype(jnp.float32)
    rescale = 1.0 / math.sqrt(NS)
    wave = jnp.sum(wavelet * chosen[None, :], axis=1) * rescale
    wave = jnp.where(core == 0, wave, -wave[::-1])
    estimate = solve(partner, place, wave, acquired, filled, second)

    returned = lax.all_to_all(estimate, BIN_AXES, split_axis=0, concat_axis=0, tiled=True)
    paired = inverse.reshape(2, NF, NT).transpose(1, 0, 2)
    tables = np.stack([paired.reshape(2 * NF, NT), paired[:, ::-1].reshape(2 * NF, NT)])
    return restore(place, returned, jnp.asarray(tables))


def solution(mesh):
    fine = Mesh(mesh.devices.reshape(2, 2, 2, 4, 4), ALL_AXES)
    return jax.shard_map(
        shards,
        mesh=fine,
        in_specs=(P(SHOT_AXES, None, None), P(), P(), P(), P()),
        out_specs=P(SHOT_AXES, None, None),
        check_vma=False,
    )
```

```python
import math

import jax
import jax.numpy as jnp
import ml_dtypes
import numpy as np
from jax import lax
from jax.experimental import pallas as pl
from jax.experimental.pallas import tpu as pltpu
from jax.sharding import Mesh
from jax.sharding import PartitionSpec as P

NS = 1024
NT = 512
NF = 32
FLO = 4
BS = 8
ITERS = 5
NB = NS // BS
NGROUPS = 8
GROUP = 32
OWN = GROUP * BS
ALL_AXES = ("z_hi", "z_lo", "core", "x", "y")
BIN_AXES = ("z_lo", "x", "y")
SHOT_AXES = ("x", "y", "z_hi", "z_lo", "core")


def dft_tables():
    sample_index = np.arange(NT, dtype=np.int32)
    bin_index = FLO + np.arange(NF, dtype=np.int32)
    angles = (bin_index[:, None] * sample_index[None, :] % NT).astype(np.float32) * np.float32(
        2.0 * math.pi / NT
    )
    cycles = np.concatenate([np.cos(angles), -np.sin(angles)], axis=0).astype(np.float32)
    forward = (cycles * np.float32(1.0 / math.sqrt(NT))).astype(ml_dtypes.bfloat16)
    inverse = (cycles * np.float32(math.sqrt(2.0 / NF))).astype(ml_dtypes.bfloat16)
    return (forward, inverse)


def source_of(block):
    return (block % 8) * 16 + block // 8


def transform_kernel(table_from, traces, out, table, held, wide, sems):
    shots = traces.shape[0]
    copies = [pltpu.make_async_copy(traces.at[s], held.at[s], sems.at[s]) for s in range(shots)]
    table_copy = pltpu.make_async_copy(table_from, table, sems.at[shots])
    table_copy.start()
    for copy in copies:
        copy.start()
    table_copy.wait()
    for s in range(shots):
        copies[s].wait()
        wide[s] = lax.dot_general(
            table[...], held[s], (((1,), (1,)), ((), ())), preferred_element_type=jnp.float32
        )
    ordered = jnp.transpose(wide[...], (1, 0, 2)).astype(jnp.bfloat16)
    out[:64] = ordered
    out[64:] = ordered


def transform(table, traces):
    vmem = pl.BlockSpec(memory_space=pltpu.VMEM)
    return pl.pallas_call(
        transform_kernel,
        out_shape=jax.ShapeDtypeStruct((NB, BS, NS), jnp.bfloat16),
        in_specs=[pl.BlockSpec(memory_space=pltpu.HBM)] * 2,
        out_specs=vmem,
        scratch_shapes=[
            pltpu.VMEM((2 * NF, NT), jnp.bfloat16),
            pltpu.VMEM((BS, NS, NT), jnp.bfloat16),
            pltpu.VMEM((BS, 2 * NF, NS), jnp.float32),
            pltpu.SemaphoreType.DMA((BS + 1,)),
        ],
        compiler_params=pltpu.CompilerParams(vmem_limit_bytes=54 * 1024 * 1024),
        name="transform",
    )(table, traces)


def restore_kernel(place, spectra, tables, out, wide, held, sems):
    wide[...] = jnp.transpose(
        spectra[...].astype(jnp.float32).reshape(2 * NF, BS, NS), (1, 0, 2)
    )
    table = tables[place[1]]
    copies = []
    for s in range(BS):
        held[s] = lax.dot_general(
            wide[s].astype(jnp.bfloat16),
            table,
            (((0,), (0,)), ((), ())),
            preferred_element_type=jnp.float32,
        ).astype(jnp.bfloat16)
        copies.append(pltpu.make_async_copy(held.at[s], out.at[s], sems.at[s]))
        copies[-1].start()
    for copy in copies:
        copy.wait()


def restore(place, spectra, tables):
    vmem = pl.BlockSpec(memory_space=pltpu.VMEM)
    return pl.pallas_call(
        restore_kernel,
        out_shape=jax.ShapeDtypeStruct((BS, NS, NT), jnp.bfloat16),
        in_specs=[pl.BlockSpec(memory_space=pltpu.SMEM), vmem, vmem],
        out_specs=pl.BlockSpec(memory_space=pltpu.HBM),
        scratch_shapes=[
            pltpu.VMEM((BS, 2 * NF, NS), jnp.float32),
            pltpu.VMEM((BS, NS, NT), jnp.bfloat16),
            pltpu.SemaphoreType.DMA((BS,)),
        ],
        compiler_params=pltpu.CompilerParams(vmem_limit_bytes=24 * 1024 * 1024),
        name="restore",
    )(place, spectra, tables)


def fill(partner, acquired, rows, mirror, mask, filled):
    column_block = lax.broadcasted_iota(jnp.int32, (NB, NS), 1) // BS
    expand = (column_block == lax.broadcasted_iota(jnp.int32, (NB, NS), 0)).astype(jnp.bfloat16)
    mask[...] = jnp.dot(
        acquired[...].astype(jnp.float32).astype(jnp.bfloat16),
        expand,
        preferred_element_type=jnp.float32,
    )
    size = 256
    identity = (
        lax.broadcasted_iota(jnp.int32, (size, size), 0)
        == lax.broadcasted_iota(jnp.int32, (size, size), 1)
    ).astype(jnp.bfloat16)
    for group in range(NS // size):
        taken = jnp.concatenate(
            [
                rows[source_of(partner[group * (size // BS) + i])].astype(jnp.float32)
                for i in range(size // BS)
            ],
            axis=0,
        ).astype(jnp.bfloat16)
        for tile in range(NS // size):
            turned = lax.dot_general(
                identity,
                taken[:, tile * size : (tile + 1) * size],
                (((1,), (1,)), ((), ())),
                preferred_element_type=jnp.float32,
            )
            mirror[
                tile * (size // BS) : (tile + 1) * (size // BS),
                :,
                group * size : (group + 1) * size,
            ] = turned.reshape(size // BS, BS, size).astype(jnp.bfloat16)

    def choose(pair, carry):
        blocks = []
        for i in range(2):
            block = pair * 2 + i
            keep = mask[pl.ds(block, 1), :] > 0.5
            blocks.append(
                jnp.where(
                    keep,
                    rows[source_of(block)].astype(jnp.float32),
                    mirror[partner[block]].astype(jnp.float32),
                )
            )
        row = pl.multiple_of(pair * 16, 16)
        filled[pl.ds(row, 16), :] = jnp.concatenate(blocks, axis=0).astype(jnp.bfloat16)
        return carry

    lax.fori_loop(0, NB // 2, choose, 0, unroll=8)


def fill_first_kernel(partner, acquired, rows, filled, mirror, mask):
    fill(partner, acquired, rows, mirror, mask, filled)


def fill_first(partner, acquired, rows):
    vmem = pl.BlockSpec(memory_space=pltpu.VMEM)
    return pl.pallas_call(
        fill_first_kernel,
        out_shape=jax.ShapeDtypeStruct((NS, NS), jnp.bfloat16),
        in_specs=[pl.BlockSpec(memory_space=pltpu.SMEM), vmem, vmem],
        out_specs=vmem,
        scratch_shapes=[
            pltpu.VMEM((NB, BS, NS), jnp.bfloat16),
            pltpu.VMEM((NB, NS), jnp.float32),
        ],
        compiler_params=pltpu.CompilerParams(vmem_limit_bytes=16 * 1024 * 1024),
        name="fill_first",
    )(partner, acquired, rows)


def solve_kernel(
    partner,
    place,
    band_counts,
    wavelet,
    acquired,
    first,
    rows,
    out,
    mirror,
    second,
    factor,
    left,
    base,
    mask,
):
    band_end = jnp.int32(0)
    group = jnp.int32(0)
    for g in range(NGROUPS):
        band_end = band_end + band_counts[g]
        group = group + (band_end <= place[2]).astype(jnp.int32)
    rescale = 1.0 / math.sqrt(NS)
    wave_re = wavelet[0, group] * rescale
    wave_im = wavelet[1, group] * rescale
    wave = (
        jnp.where(place[1] == 0, wave_re, -wave_im),
        jnp.where(place[1] == 0, wave_im, -wave_re),
    )
    fill(partner, acquired, rows, mirror, mask, second)

    def scale(pair, carry):
        row = pl.multiple_of(pair * 16, 16)
        real = first[pl.ds(row, 16), :].astype(jnp.float32)
        imag = second[pl.ds(row, 16), :].astype(jnp.float32)
        factor[pl.ds(row, 16), :] = (wave[0] * real - wave[1] * imag).astype(jnp.bfloat16)
        factor[pl.ds(NS + row, 16), :] = (wave[0] * imag + wave[1] * real).astype(jnp.bfloat16)
        return carry

    lax.fori_loop(0, NB // 2, scale, 0, unroll=8)

    def put(slot, row, rows, real, imag, column, columns):
        real_low = real.astype(jnp.bfloat16)
        imag_low = imag.astype(jnp.bfloat16)
        left[slot, pl.ds(row, rows), pl.ds(column, columns)] = real_low
        left[slot, pl.ds(row, rows), pl.ds(NS + column, columns)] = -imag_low
        left[slot, pl.ds(OWN + row, rows), pl.ds(column, columns)] = imag_low
        left[slot, pl.ds(OWN + row, rows), pl.ds(NS + column, columns)] = real_low

    def own(pair, carry):
        values = []
        for part in (first, second):
            blocks = []
            for i in range(2):
                member = pair * 2 + i
                chip = (member % 16) * 4 + member // 16 + place[0]
                both = part[pl.ds(pl.multiple_of(chip * 16, 16), 16), :].astype(jnp.float32)
                blocks.append(jnp.where(place[1] == 0, both[:BS], both[BS:]))
            values.append(jnp.concatenate(blocks, axis=0))
        row = pl.multiple_of(pair * 16, 16)
        base[pl.ds(row, 16), :] = values[0]
        base[pl.ds(OWN + row, 16), :] = values[1]
        put(0, row, 16, values[0], values[1], 0, NS)
        return carry

    lax.fori_loop(0, GROUP // 2, own, 0, unroll=4)

    width = 256

    def sweep(slot, last):
        for tile in range(NS // width):
            columns = pl.ds(tile * width, width)
            product = jnp.dot(
                left[slot], factor[:, columns], preferred_element_type=jnp.float32
            )
            value = base[:, columns] - product
            if last:
                out[:, 0, :, columns] = (
                    value[:OWN].reshape(GROUP, BS, width).astype(jnp.bfloat16)
                )
                out[:, 1, :, columns] = (
                    value[OWN:].reshape(GROUP, BS, width).astype(jnp.bfloat16)
                )
            else:
                put(1 - slot, 0, OWN, value[:OWN], value[OWN:], tile * width, width)

    for turn_index in range(ITERS):
        sweep(turn_index % 2, turn_index == ITERS - 1)


def solve(partner, place, band_counts, wavelet, acquired, first, rows):
    smem = pl.BlockSpec(memory_space=pltpu.SMEM)
    vmem = pl.BlockSpec(memory_space=pltpu.VMEM)
    return pl.pallas_call(
        solve_kernel,
        out_shape=jax.ShapeDtypeStruct((GROUP, 2, BS, NS), jnp.bfloat16),
        in_specs=[smem, smem, smem, smem, vmem, vmem, vmem],
        out_specs=vmem,
        scratch_shapes=[
            pltpu.VMEM((NB, BS, NS), jnp.bfloat16),
            pltpu.VMEM((NS, NS), jnp.bfloat16),
            pltpu.VMEM((2 * NS, NS), jnp.bfloat16),
            pltpu.VMEM((2, 2 * OWN, 2 * NS), jnp.bfloat16),
            pltpu.VMEM((2 * OWN, NS), jnp.float32),
            pltpu.VMEM((NB, NS), jnp.float32),
        ],
        compiler_params=pltpu.CompilerParams(vmem_limit_bytes=32 * 1024 * 1024),
        name="solve",
    )(partner, place, band_counts, wavelet, acquired, first, rows)


def shards(recorded, acquired, partner, band_counts, wavelet):
    core = lax.axis_index("core")
    z_hi = lax.axis_index("z_hi")
    my_bin = lax.axis_index("z_lo") * 16 + lax.axis_index("x") * 4 + lax.axis_index("y")
    place = jnp.stack([z_hi * 2, core, my_bin]).astype(jnp.int32)
    forward, inverse = dft_tables()
    ordered = forward.reshape(2, 2, 16, NT).transpose(1, 0, 2, 3).reshape(2 * NF, NT)
    outgoing = transform(jnp.asarray(ordered), recorded)
    first = lax.all_to_all(outgoing, ALL_AXES, split_axis=0, concat_axis=0, tiled=True)
    second = lax.ppermute(first, "core", [(0, 1), (1, 0)])
    filled = fill_first(partner, acquired, first)

    estimate = solve(partner, place, band_counts, wavelet, acquired, filled, second)

    returned = lax.all_to_all(estimate, BIN_AXES, split_axis=0, concat_axis=0, tiled=True)
    paired = inverse.reshape(2, NF, NT).transpose(1, 0, 2)
    tables = np.stack([paired.reshape(2 * NF, NT), paired[:, ::-1].reshape(2 * NF, NT)])
    return restore(place, returned, jnp.asarray(tables))


def solution(mesh):
    fine = Mesh(mesh.devices.reshape(2, 2, 2, 4, 4), ALL_AXES)
    return jax.shard_map(
        shards,
        mesh=fine,
        in_specs=(P(SHOT_AXES, None, None), P(), P(), P(), P()),
        out_specs=P(SHOT_AXES, None, None),
        check_vma=False,
    )
```

```python
import math

import jax
import jax.numpy as jnp
import ml_dtypes
import numpy as np
from jax import lax
from jax.experimental import pallas as pl
from jax.experimental.pallas import tpu as pltpu
from jax.sharding import Mesh
from jax.sharding import PartitionSpec as P

NS = 1024
NT = 512
NF = 32
FLO = 4
BS = 8
ITERS = 5
NB = NS // BS
NGROUPS = 8
GROUP = 32
OWN = GROUP * BS
ALL_AXES = ("z_hi", "z_lo", "core", "x", "y")
BIN_AXES = ("z_lo", "x", "y")
SHOT_AXES = ("x", "y", "z_hi", "z_lo", "core")


def dft_tables():
    sample_index = np.arange(NT, dtype=np.int32)
    bin_index = FLO + np.arange(NF, dtype=np.int32)
    angles = (bin_index[:, None] * sample_index[None, :] % NT).astype(np.float32) * np.float32(
        2.0 * math.pi / NT
    )
    cycles = np.concatenate([np.cos(angles), -np.sin(angles)], axis=0).astype(np.float32)
    forward = (cycles * np.float32(1.0 / math.sqrt(NT))).astype(ml_dtypes.bfloat16)
    inverse = (cycles * np.float32(math.sqrt(2.0 / NF))).astype(ml_dtypes.bfloat16)
    return (forward, inverse)


def source_of(block):
    return (block % 8) * 16 + block // 8


def transform_kernel(table_from, traces, out, table, held, wide, sems):
    shots = traces.shape[0]
    copies = [pltpu.make_async_copy(traces.at[s], held.at[s], sems.at[s]) for s in range(shots)]
    table_copy = pltpu.make_async_copy(table_from, table, sems.at[shots])
    table_copy.start()
    for copy in copies:
        copy.start()
    table_copy.wait()
    for s in range(shots):
        copies[s].wait()
        wide[s] = lax.dot_general(
            table[...], held[s], (((1,), (1,)), ((), ())), preferred_element_type=jnp.float32
        )
    ordered = jnp.transpose(wide[...], (1, 0, 2)).astype(jnp.bfloat16)
    out[:64] = ordered
    out[64:] = ordered


def transform(table, traces):
    vmem = pl.BlockSpec(memory_space=pltpu.VMEM)
    return pl.pallas_call(
        transform_kernel,
        out_shape=jax.ShapeDtypeStruct((NB, BS, NS), jnp.bfloat16),
        in_specs=[pl.BlockSpec(memory_space=pltpu.HBM)] * 2,
        out_specs=vmem,
        scratch_shapes=[
            pltpu.VMEM((2 * NF, NT), jnp.bfloat16),
            pltpu.VMEM((BS, NS, NT), jnp.bfloat16),
            pltpu.VMEM((BS, 2 * NF, NS), jnp.float32),
            pltpu.SemaphoreType.DMA((BS + 1,)),
        ],
        compiler_params=pltpu.CompilerParams(vmem_limit_bytes=54 * 1024 * 1024),
        name="transform",
    )(table, traces)


def restore_kernel(place, spectra, tables, out, wide, held, sems):
    wide[...] = jnp.transpose(
        spectra[...].astype(jnp.float32).reshape(2 * NF, BS, NS), (1, 0, 2)
    )
    table = tables[place[1]]
    copies = []
    for s in range(BS):
        held[s] = lax.dot_general(
            wide[s].astype(jnp.bfloat16),
            table,
            (((0,), (0,)), ((), ())),
            preferred_element_type=jnp.float32,
        ).astype(jnp.bfloat16)
        copies.append(pltpu.make_async_copy(held.at[s], out.at[s], sems.at[s]))
        copies[-1].start()
    for copy in copies:
        copy.wait()


def restore(place, spectra, tables):
    vmem = pl.BlockSpec(memory_space=pltpu.VMEM)
    return pl.pallas_call(
        restore_kernel,
        out_shape=jax.ShapeDtypeStruct((BS, NS, NT), jnp.bfloat16),
        in_specs=[pl.BlockSpec(memory_space=pltpu.SMEM), vmem, vmem],
        out_specs=pl.BlockSpec(memory_space=pltpu.HBM),
        scratch_shapes=[
            pltpu.VMEM((BS, 2 * NF, NS), jnp.float32),
            pltpu.VMEM((BS, NS, NT), jnp.bfloat16),
            pltpu.SemaphoreType.DMA((BS,)),
        ],
        compiler_params=pltpu.CompilerParams(vmem_limit_bytes=24 * 1024 * 1024),
        name="restore",
    )(place, spectra, tables)


def spread(acquired, mask):
    column_block = lax.broadcasted_iota(jnp.int32, (NB, NS), 1) // BS
    expand = (column_block == lax.broadcasted_iota(jnp.int32, (NB, NS), 0)).astype(jnp.bfloat16)
    mask[...] = jnp.dot(
        acquired[...].astype(jnp.float32).astype(jnp.bfloat16),
        expand,
        preferred_element_type=jnp.float32,
    )


def turn(partner, rows, mirror):
    size = 256
    identity = (
        lax.broadcasted_iota(jnp.int32, (size, size), 0)
        == lax.broadcasted_iota(jnp.int32, (size, size), 1)
    ).astype(jnp.bfloat16)
    for group in range(NS // size):
        taken = jnp.concatenate(
            [
                rows[source_of(partner[group * (size // BS) + i])].astype(jnp.float32)
                for i in range(size // BS)
            ],
            axis=0,
        ).astype(jnp.bfloat16)
        for tile in range(NS // size):
            turned = lax.dot_general(
                identity,
                taken[:, tile * size : (tile + 1) * size],
                (((1,), (1,)), ((), ())),
                preferred_element_type=jnp.float32,
            )
            mirror[
                tile * (size // BS) : (tile + 1) * (size // BS),
                :,
                group * size : (group + 1) * size,
            ] = turned.reshape(size // BS, BS, size).astype(jnp.bfloat16)


def choose(partner, rows, mirror, mask, block, columns):
    keep = mask[pl.ds(block, 1), columns] > 0.5
    return jnp.where(
        keep,
        rows[source_of(block), :, columns].astype(jnp.float32),
        mirror[partner[block], :, columns].astype(jnp.float32),
    )


def fill_first_kernel(partner, acquired, rows, filled, mirror, mask):
    spread(acquired, mask)
    turn(partner, rows, mirror)

    def pick(pair, carry):
        blocks = [
            choose(partner, rows, mirror, mask, pair * 2 + i, slice(None)) for i in range(2)
        ]
        row = pl.multiple_of(pair * 16, 16)
        filled[pl.ds(row, 16), :] = jnp.concatenate(blocks, axis=0).astype(jnp.bfloat16)
        return carry

    lax.fori_loop(0, NB // 2, pick, 0, unroll=8)


def fill_first(partner, acquired, rows):
    vmem = pl.BlockSpec(memory_space=pltpu.VMEM)
    return pl.pallas_call(
        fill_first_kernel,
        out_shape=jax.ShapeDtypeStruct((NS, NS), jnp.bfloat16),
        in_specs=[pl.BlockSpec(memory_space=pltpu.SMEM), vmem, vmem],
        out_specs=vmem,
        scratch_shapes=[
            pltpu.VMEM((NB, BS, NS), jnp.bfloat16),
            pltpu.VMEM((NB, NS), jnp.float32),
        ],
        compiler_params=pltpu.CompilerParams(vmem_limit_bytes=16 * 1024 * 1024),
        name="fill_first",
    )(partner, acquired, rows)


def solve_kernel(
    partner,
    place,
    band_counts,
    wavelet,
    acquired,
    first,
    rows,
    out,
    mirror,
    factor,
    left,
    base,
    mask,
):
    band_end = jnp.int32(0)
    group = jnp.int32(0)
    for g in range(NGROUPS):
        band_end = band_end + band_counts[g]
        group = group + (band_end <= place[2]).astype(jnp.int32)
    rescale = 1.0 / math.sqrt(NS)
    wave_re = wavelet[0, group] * rescale
    wave_im = wavelet[1, group] * rescale
    wave = (
        jnp.where(place[1] == 0, wave_re, -wave_im),
        jnp.where(place[1] == 0, wave_im, -wave_re),
    )
    spread(acquired, mask)
    turn(partner, rows, mirror)

    def scale(columns):
        for pair in range(NB // 2):
            row = pair * 16
            real = first[row : row + 16, columns].astype(jnp.float32)
            imag = jnp.concatenate(
                [choose(partner, rows, mirror, mask, pair * 2 + i, columns) for i in range(2)],
                axis=0,
            )
            factor[row : row + 16, columns] = (wave[0] * real - wave[1] * imag).astype(
                jnp.bfloat16
            )
            factor[NS + row : NS + row + 16, columns] = (
                wave[0] * imag + wave[1] * real
            ).astype(jnp.bfloat16)

    def put(slot, row, rows, real, imag, column, columns):
        real_low = real.astype(jnp.bfloat16)
        imag_low = imag.astype(jnp.bfloat16)
        left[slot, pl.ds(row, rows), pl.ds(column, columns)] = real_low
        left[slot, pl.ds(row, rows), pl.ds(NS + column, columns)] = -imag_low
        left[slot, pl.ds(OWN + row, rows), pl.ds(column, columns)] = imag_low
        left[slot, pl.ds(OWN + row, rows), pl.ds(NS + column, columns)] = real_low

    def own(pair, carry):
        reals, imags = [], []
        for i in range(2):
            member = pair * 2 + i
            chip = (member % 16) * 4 + member // 16 + place[0]
            both = first[pl.ds(pl.multiple_of(chip * 16, 16), 16), :].astype(jnp.float32)
            reals.append(jnp.where(place[1] == 0, both[:BS], both[BS:]))
            imags.append(
                choose(partner, rows, mirror, mask, chip * 2 + place[1], slice(None))
            )
        real = jnp.concatenate(reals, axis=0)
        imag = jnp.concatenate(imags, axis=0)
        row = pl.multiple_of(pair * 16, 16)
        base[pl.ds(row, 16), :] = real
        base[pl.ds(OWN + row, 16), :] = imag
        put(0, row, 16, real, imag, 0, NS)
        return carry

    lax.fori_loop(0, GROUP // 2, own, 0, unroll=4)

    width = 256

    def sweep(slot, first_turn, last):
        for tile in range(NS // width):
            columns = slice(tile * width, (tile + 1) * width)
            if first_turn:
                scale(columns)
            product = jnp.dot(
                left[slot], factor[:, columns], preferred_element_type=jnp.float32
            )
            value = base[:, columns] - product
            if last:
                out[:, 0, :, columns] = (
                    value[:OWN].reshape(GROUP, BS, width).astype(jnp.bfloat16)
                )
                out[:, 1, :, columns] = (
                    value[OWN:].reshape(GROUP, BS, width).astype(jnp.bfloat16)
                )
            else:
                put(1 - slot, 0, OWN, value[:OWN], value[OWN:], tile * width, width)

    for turn_index in range(ITERS):
        sweep(turn_index % 2, turn_index == 0, turn_index == ITERS - 1)


def solve(partner, place, band_counts, wavelet, acquired, first, rows):
    smem = pl.BlockSpec(memory_space=pltpu.SMEM)
    vmem = pl.BlockSpec(memory_space=pltpu.VMEM)
    return pl.pallas_call(
        solve_kernel,
        out_shape=jax.ShapeDtypeStruct((GROUP, 2, BS, NS), jnp.bfloat16),
        in_specs=[smem, smem, smem, smem, vmem, vmem, vmem],
        out_specs=vmem,
        scratch_shapes=[
            pltpu.VMEM((NB, BS, NS), jnp.bfloat16),
            pltpu.VMEM((2 * NS, NS), jnp.bfloat16),
            pltpu.VMEM((2, 2 * OWN, 2 * NS), jnp.bfloat16),
            pltpu.VMEM((2 * OWN, NS), jnp.float32),
            pltpu.VMEM((NB, NS), jnp.float32),
        ],
        compiler_params=pltpu.CompilerParams(vmem_limit_bytes=32 * 1024 * 1024),
        name="solve",
    )(partner, place, band_counts, wavelet, acquired, first, rows)


def shards(recorded, acquired, partner, band_counts, wavelet):
    core = lax.axis_index("core")
    z_hi = lax.axis_index("z_hi")
    my_bin = lax.axis_index("z_lo") * 16 + lax.axis_index("x") * 4 + lax.axis_index("y")
    place = jnp.stack([z_hi * 2, core, my_bin]).astype(jnp.int32)
    forward, inverse = dft_tables()
    ordered = forward.reshape(2, 2, 16, NT).transpose(1, 0, 2, 3).reshape(2 * NF, NT)
    outgoing = transform(jnp.asarray(ordered), recorded)
    first = lax.all_to_all(outgoing, ALL_AXES, split_axis=0, concat_axis=0, tiled=True)
    second = lax.ppermute(first, "core", [(0, 1), (1, 0)])
    filled = fill_first(partner, acquired, first)

    estimate = solve(partner, place, band_counts, wavelet, acquired, filled, second)

    returned = lax.all_to_all(estimate, BIN_AXES, split_axis=0, concat_axis=0, tiled=True)
    paired = inverse.reshape(2, NF, NT).transpose(1, 0, 2)
    tables = np.stack([paired.reshape(2 * NF, NT), paired[:, ::-1].reshape(2 * NF, NT)])
    return restore(place, returned, jnp.asarray(tables))


def solution(mesh):
    fine = Mesh(mesh.devices.reshape(2, 2, 2, 4, 4), ALL_AXES)
    return jax.shard_map(
        shards,
        mesh=fine,
        in_specs=(P(SHOT_AXES, None, None), P(), P(), P(), P()),
        out_specs=P(SHOT_AXES, None, None),
        check_vma=False,
    )
```

```python
import math

import jax
import jax.numpy as jnp
import ml_dtypes
import numpy as np
from jax import lax
from jax.experimental import pallas as pl
from jax.experimental.pallas import tpu as pltpu
from jax.sharding import Mesh
from jax.sharding import PartitionSpec as P

NS = 1024
NT = 512
NF = 32
FLO = 4
BS = 8
ITERS = 5
NB = NS // BS
NGROUPS = 8
GROUP = 32
OWN = GROUP * BS
ALL_AXES = ("z_hi", "z_lo", "core", "x", "y")
BIN_AXES = ("z_lo", "x", "y")
SHOT_AXES = ("x", "y", "z_hi", "z_lo", "core")


def dft_tables():
    sample_index = np.arange(NT, dtype=np.int32)
    bin_index = FLO + np.arange(NF, dtype=np.int32)
    angles = (bin_index[:, None] * sample_index[None, :] % NT).astype(np.float32) * np.float32(
        2.0 * math.pi / NT
    )
    cycles = np.concatenate([np.cos(angles), -np.sin(angles)], axis=0).astype(np.float32)
    forward = (cycles * np.float32(1.0 / math.sqrt(NT))).astype(ml_dtypes.bfloat16)
    inverse = (cycles * np.float32(math.sqrt(2.0 / NF))).astype(ml_dtypes.bfloat16)
    return (forward, inverse)


def source_of(block):
    return (block % 8) * 16 + block // 8


def transform_kernel(table_from, traces, out, table, held, wide, sems):
    shots = traces.shape[0]
    copies = [pltpu.make_async_copy(traces.at[s], held.at[s], sems.at[s]) for s in range(shots)]
    table_copy = pltpu.make_async_copy(table_from, table, sems.at[shots])
    table_copy.start()
    for copy in copies:
        copy.start()
    table_copy.wait()
    for s in range(shots):
        copies[s].wait()
        wide[s] = lax.dot_general(
            table[...], held[s], (((1,), (1,)), ((), ())), preferred_element_type=jnp.float32
        )
    ordered = jnp.transpose(wide[...], (1, 0, 2)).astype(jnp.bfloat16)
    out[:64] = ordered
    out[64:] = ordered


def transform(table, traces):
    vmem = pl.BlockSpec(memory_space=pltpu.VMEM)
    return pl.pallas_call(
        transform_kernel,
        out_shape=jax.ShapeDtypeStruct((NB, BS, NS), jnp.bfloat16),
        in_specs=[pl.BlockSpec(memory_space=pltpu.HBM)] * 2,
        out_specs=vmem,
        scratch_shapes=[
            pltpu.VMEM((2 * NF, NT), jnp.bfloat16),
            pltpu.VMEM((BS, NS, NT), jnp.bfloat16),
            pltpu.VMEM((BS, 2 * NF, NS), jnp.float32),
            pltpu.SemaphoreType.DMA((BS + 1,)),
        ],
        compiler_params=pltpu.CompilerParams(vmem_limit_bytes=24 * 1024 * 1024),
        name="transform",
    )(table, traces)


def restore_kernel(place, spectra, tables, out, wide, held, sems):
    wide[...] = jnp.transpose(
        spectra[...].astype(jnp.float32).reshape(2 * NF, BS, NS), (1, 0, 2)
    )
    table = tables[place[1]]
    copies = []
    for s in range(BS):
        held[s] = lax.dot_general(
            wide[s].astype(jnp.bfloat16),
            table,
            (((0,), (0,)), ((), ())),
            preferred_element_type=jnp.float32,
        ).astype(jnp.bfloat16)
        copies.append(pltpu.make_async_copy(held.at[s], out.at[s], sems.at[s]))
        copies[-1].start()
    for copy in copies:
        copy.wait()


def restore(place, spectra, tables):
    vmem = pl.BlockSpec(memory_space=pltpu.VMEM)
    return pl.pallas_call(
        restore_kernel,
        out_shape=jax.ShapeDtypeStruct((BS, NS, NT), jnp.bfloat16),
        in_specs=[pl.BlockSpec(memory_space=pltpu.SMEM), vmem, vmem],
        out_specs=pl.BlockSpec(memory_space=pltpu.HBM),
        scratch_shapes=[
            pltpu.VMEM((BS, 2 * NF, NS), jnp.float32),
            pltpu.VMEM((BS, NS, NT), jnp.bfloat16),
            pltpu.SemaphoreType.DMA((BS,)),
        ],
        compiler_params=pltpu.CompilerParams(vmem_limit_bytes=24 * 1024 * 1024),
        name="restore",
    )(place, spectra, tables)


def spread(acquired, mask):
    column_block = lax.broadcasted_iota(jnp.int32, (NB, NS), 1) // BS
    expand = (column_block == lax.broadcasted_iota(jnp.int32, (NB, NS), 0)).astype(jnp.bfloat16)
    mask[...] = jnp.dot(
        acquired[...].astype(jnp.float32).astype(jnp.bfloat16),
        expand,
        preferred_element_type=jnp.float32,
    )


def turn(partner, rows, mirror):
    size = 256
    identity = (
        lax.broadcasted_iota(jnp.int32, (size, size), 0)
        == lax.broadcasted_iota(jnp.int32, (size, size), 1)
    ).astype(jnp.bfloat16)
    for group in range(NS // size):
        taken = jnp.concatenate(
            [
                rows[source_of(partner[group * (size // BS) + i])].astype(jnp.float32)
                for i in range(size // BS)
            ],
            axis=0,
        ).astype(jnp.bfloat16)
        for tile in range(NS // size):
            turned = lax.dot_general(
                identity,
                taken[:, tile * size : (tile + 1) * size],
                (((1,), (1,)), ((), ())),
                preferred_element_type=jnp.float32,
            )
            mirror[
                tile * (size // BS) : (tile + 1) * (size // BS),
                :,
                group * size : (group + 1) * size,
            ] = turned.reshape(size // BS, BS, size).astype(jnp.bfloat16)


def choose(partner, rows, mirror, mask, block, columns):
    keep = mask[pl.ds(block, 1), columns] > 0.5
    return jnp.where(
        keep,
        rows[source_of(block), :, columns].astype(jnp.float32),
        mirror[partner[block], :, columns].astype(jnp.float32),
    )


def fill_first_kernel(partner, acquired, rows, filled, mask, mirror):
    spread(acquired, mask)
    turn(partner, rows, mirror)

    def pick(pair, carry):
        blocks = [
            choose(partner, rows, mirror, mask, pair * 2 + i, slice(None)) for i in range(2)
        ]
        row = pl.multiple_of(pair * 16, 16)
        filled[pl.ds(row, 16), :] = jnp.concatenate(blocks, axis=0).astype(jnp.bfloat16)
        return carry

    lax.fori_loop(0, NB // 2, pick, 0, unroll=8)


def fill_first(partner, acquired, rows):
    vmem = pl.BlockSpec(memory_space=pltpu.VMEM)
    return pl.pallas_call(
        fill_first_kernel,
        out_shape=(
            jax.ShapeDtypeStruct((NS, NS), jnp.bfloat16),
            jax.ShapeDtypeStruct((NB, NS), jnp.float32),
        ),
        in_specs=[pl.BlockSpec(memory_space=pltpu.SMEM), vmem, vmem],
        out_specs=(vmem, vmem),
        scratch_shapes=[pltpu.VMEM((NB, BS, NS), jnp.bfloat16)],
        compiler_params=pltpu.CompilerParams(vmem_limit_bytes=16 * 1024 * 1024),
        name="fill_first",
    )(partner, acquired, rows)


def solve_kernel(
    partner,
    place,
    band_counts,
    wavelet,
    mask,
    first,
    rows,
    out,
    mirror,
    factor,
    left,
    base,
):
    band_end = jnp.int32(0)
    group = jnp.int32(0)
    for g in range(NGROUPS):
        band_end = band_end + band_counts[g]
        group = group + (band_end <= place[2]).astype(jnp.int32)
    rescale = 1.0 / math.sqrt(NS)
    wave_re = wavelet[0, group] * rescale
    wave_im = wavelet[1, group] * rescale
    wave = (
        jnp.where(place[1] == 0, wave_re, -wave_im),
        jnp.where(place[1] == 0, wave_im, -wave_re),
    )
    turn(partner, rows, mirror)

    def scale(columns):
        for pair in range(NB // 2):
            row = pair * 16
            real = first[row : row + 16, columns].astype(jnp.float32)
            imag = jnp.concatenate(
                [choose(partner, rows, mirror, mask, pair * 2 + i, columns) for i in range(2)],
                axis=0,
            )
            factor[row : row + 16, columns] = (wave[0] * real - wave[1] * imag).astype(
                jnp.bfloat16
            )
            factor[NS + row : NS + row + 16, columns] = (
                wave[0] * imag + wave[1] * real
            ).astype(jnp.bfloat16)

    def put(slot, row, rows, real, imag, column, columns):
        real_low = real.astype(jnp.bfloat16)
        imag_low = imag.astype(jnp.bfloat16)
        left[slot, pl.ds(row, rows), pl.ds(column, columns)] = real_low
        left[slot, pl.ds(row, rows), pl.ds(NS + column, columns)] = -imag_low
        left[slot, pl.ds(OWN + row, rows), pl.ds(column, columns)] = imag_low
        left[slot, pl.ds(OWN + row, rows), pl.ds(NS + column, columns)] = real_low

    def own(pair, carry):
        reals, imags = [], []
        for i in range(2):
            member = pair * 2 + i
            chip = (member % 16) * 4 + member // 16 + place[0]
            both = first[pl.ds(pl.multiple_of(chip * 16, 16), 16), :].astype(jnp.float32)
            reals.append(jnp.where(place[1] == 0, both[:BS], both[BS:]))
            imags.append(
                choose(partner, rows, mirror, mask, chip * 2 + place[1], slice(None))
            )
        real = jnp.concatenate(reals, axis=0)
        imag = jnp.concatenate(imags, axis=0)
        row = pl.multiple_of(pair * 16, 16)
        base[pl.ds(row, 16), :] = real
        base[pl.ds(OWN + row, 16), :] = imag
        put(0, row, 16, real, imag, 0, NS)
        return carry

    lax.fori_loop(0, GROUP // 2, own, 0, unroll=4)

    width = 256

    def sweep(slot, first_turn, last):
        for tile in range(NS // width):
            columns = slice(tile * width, (tile + 1) * width)
            if first_turn:
                scale(columns)
            product = jnp.dot(
                left[slot], factor[:, columns], preferred_element_type=jnp.float32
            )
            value = base[:, columns] - product
            if last:
                out[:, 0, :, columns] = (
                    value[:OWN].reshape(GROUP, BS, width).astype(jnp.bfloat16)
                )
                out[:, 1, :, columns] = (
                    value[OWN:].reshape(GROUP, BS, width).astype(jnp.bfloat16)
                )
            else:
                put(1 - slot, 0, OWN, value[:OWN], value[OWN:], tile * width, width)

    for turn_index in range(ITERS):
        sweep(turn_index % 2, turn_index == 0, turn_index == ITERS - 1)


def solve(partner, place, band_counts, wavelet, mask, first, rows):
    smem = pl.BlockSpec(memory_space=pltpu.SMEM)
    vmem = pl.BlockSpec(memory_space=pltpu.VMEM)
    return pl.pallas_call(
        solve_kernel,
        out_shape=jax.ShapeDtypeStruct((GROUP, 2, BS, NS), jnp.bfloat16),
        in_specs=[smem, smem, smem, smem, vmem, vmem, vmem],
        out_specs=vmem,
        scratch_shapes=[
            pltpu.VMEM((NB, BS, NS), jnp.bfloat16),
            pltpu.VMEM((2 * NS, NS), jnp.bfloat16),
            pltpu.VMEM((2, 2 * OWN, 2 * NS), jnp.bfloat16),
            pltpu.VMEM((2 * OWN, NS), jnp.float32),
        ],
        compiler_params=pltpu.CompilerParams(vmem_limit_bytes=32 * 1024 * 1024),
        name="solve",
    )(partner, place, band_counts, wavelet, mask, first, rows)


def shards(recorded, acquired, partner, band_counts, wavelet):
    core = lax.axis_index("core")
    z_hi = lax.axis_index("z_hi")
    my_bin = lax.axis_index("z_lo") * 16 + lax.axis_index("x") * 4 + lax.axis_index("y")
    place = jnp.stack([z_hi * 2, core, my_bin]).astype(jnp.int32)
    forward, inverse = dft_tables()
    ordered = forward.reshape(2, 2, 16, NT).transpose(1, 0, 2, 3).reshape(2 * NF, NT)
    outgoing = transform(
        pltpu.with_memory_space_constraint(jnp.asarray(ordered), pltpu.HBM),
        pltpu.with_memory_space_constraint(recorded, pltpu.HBM),
    )
    first = lax.all_to_all(outgoing, ALL_AXES, split_axis=0, concat_axis=0, tiled=True)
    second = lax.ppermute(first, "core", [(0, 1), (1, 0)])
    filled, mask = fill_first(partner, acquired, first)

    estimate = solve(partner, place, band_counts, wavelet, mask, filled, second)

    returned = lax.all_to_all(estimate, BIN_AXES, split_axis=0, concat_axis=0, tiled=True)
    paired = inverse.reshape(2, NF, NT).transpose(1, 0, 2)
    tables = np.stack([paired.reshape(2 * NF, NT), paired[:, ::-1].reshape(2 * NF, NT)])
    return restore(place, returned, jnp.asarray(tables))


def solution(mesh):
    fine = Mesh(mesh.devices.reshape(2, 2, 2, 4, 4), ALL_AXES)
    return jax.shard_map(
        shards,
        mesh=fine,
        in_specs=(P(SHOT_AXES, None, None), P(), P(), P(), P()),
        out_specs=P(SHOT_AXES, None, None),
        check_vma=False,
    )
```

```python
import math

import jax
import jax.numpy as jnp
import ml_dtypes
import numpy as np
from jax import lax
from jax.experimental import pallas as pl
from jax.experimental.pallas import tpu as pltpu
from jax.sharding import Mesh
from jax.sharding import PartitionSpec as P

NS = 1024
NT = 512
NF = 32
FLO = 4
BS = 8
ITERS = 5
NB = NS // BS
NGROUPS = 8
GROUP = 32
OWN = GROUP * BS
ALL_AXES = ("z_hi", "z_lo", "core", "x", "y")
BIN_AXES = ("z_lo", "x", "y")
SHOT_AXES = ("x", "y", "z_hi", "z_lo", "core")


def dft_tables():
    sample_index = np.arange(NT, dtype=np.int32)
    bin_index = FLO + np.arange(NF, dtype=np.int32)
    angles = (bin_index[:, None] * sample_index[None, :] % NT).astype(np.float32) * np.float32(
        2.0 * math.pi / NT
    )
    cycles = np.concatenate([np.cos(angles), -np.sin(angles)], axis=0).astype(np.float32)
    forward = (cycles * np.float32(1.0 / math.sqrt(NT))).astype(ml_dtypes.bfloat16)
    inverse = (cycles * np.float32(math.sqrt(2.0 / NF))).astype(ml_dtypes.bfloat16)
    return (forward, inverse)


def source_of(block):
    return (block % 8) * 16 + block // 8


def transform_kernel(table_from, traces, out, table, held, wide, sems):
    shots = traces.shape[0]
    copies = [pltpu.make_async_copy(traces.at[s], held.at[s], sems.at[s]) for s in range(shots)]
    table_copy = pltpu.make_async_copy(table_from, table, sems.at[shots])
    table_copy.start()
    for copy in copies:
        copy.start()
    table_copy.wait()
    for s in range(shots):
        copies[s].wait()
        wide[s] = lax.dot_general(
            table[...], held[s], (((1,), (1,)), ((), ())), preferred_element_type=jnp.float32
        )
    ordered = jnp.transpose(wide[...], (1, 0, 2)).astype(jnp.bfloat16)
    out[:64] = ordered
    out[64:] = ordered


def transform(table, traces):
    vmem = pl.BlockSpec(memory_space=pltpu.VMEM)
    return pl.pallas_call(
        transform_kernel,
        out_shape=jax.ShapeDtypeStruct((NB, BS, NS), jnp.bfloat16),
        in_specs=[pl.BlockSpec(memory_space=pltpu.HBM)] * 2,
        out_specs=vmem,
        scratch_shapes=[
            pltpu.VMEM((2 * NF, NT), jnp.bfloat16),
            pltpu.VMEM((BS, NS, NT), jnp.bfloat16),
            pltpu.VMEM((BS, 2 * NF, NS), jnp.float32),
            pltpu.SemaphoreType.DMA((BS + 1,)),
        ],
        compiler_params=pltpu.CompilerParams(vmem_limit_bytes=24 * 1024 * 1024),
        name="transform",
    )(table, traces)


def restore_kernel(place, spectra, tables, out, wide, held, sems):
    wide[...] = jnp.transpose(
        spectra[...].astype(jnp.float32).reshape(2 * NF, BS, NS), (1, 0, 2)
    )
    table = tables[place[1]]
    copies = []
    for s in range(BS):
        held[s] = lax.dot_general(
            wide[s].astype(jnp.bfloat16),
            table,
            (((0,), (0,)), ((), ())),
            preferred_element_type=jnp.float32,
        ).astype(jnp.bfloat16)
        copies.append(pltpu.make_async_copy(held.at[s], out.at[s], sems.at[s]))
        copies[-1].start()
    for copy in copies:
        copy.wait()


def restore(place, spectra, tables):
    vmem = pl.BlockSpec(memory_space=pltpu.VMEM)
    return pl.pallas_call(
        restore_kernel,
        out_shape=jax.ShapeDtypeStruct((BS, NS, NT), jnp.bfloat16),
        in_specs=[pl.BlockSpec(memory_space=pltpu.SMEM), vmem, vmem],
        out_specs=pl.BlockSpec(memory_space=pltpu.HBM),
        scratch_shapes=[
            pltpu.VMEM((BS, 2 * NF, NS), jnp.float32),
            pltpu.VMEM((BS, NS, NT), jnp.bfloat16),
            pltpu.SemaphoreType.DMA((BS,)),
        ],
        compiler_params=pltpu.CompilerParams(vmem_limit_bytes=24 * 1024 * 1024),
        name="restore",
    )(place, spectra, tables)


def spread(acquired, mask):
    column_block = lax.broadcasted_iota(jnp.int32, (NB, NS), 1) // BS
    expand = (column_block == lax.broadcasted_iota(jnp.int32, (NB, NS), 0)).astype(jnp.bfloat16)
    mask[...] = jnp.dot(
        acquired[...].astype(jnp.float32).astype(jnp.bfloat16),
        expand,
        preferred_element_type=jnp.float32,
    )


def turn(partner, rows, mirror):
    size = 256
    identity = (
        lax.broadcasted_iota(jnp.int32, (size, size), 0)
        == lax.broadcasted_iota(jnp.int32, (size, size), 1)
    ).astype(jnp.bfloat16)
    for group in range(NS // size):
        taken = jnp.concatenate(
            [
                rows[source_of(partner[group * (size // BS) + i])].astype(jnp.float32)
                for i in range(size // BS)
            ],
            axis=0,
        ).astype(jnp.bfloat16)
        for tile in range(NS // size):
            turned = lax.dot_general(
                identity,
                taken[:, tile * size : (tile + 1) * size],
                (((1,), (1,)), ((), ())),
                preferred_element_type=jnp.float32,
            )
            mirror[
                tile * (size // BS) : (tile + 1) * (size // BS),
                :,
                group * size : (group + 1) * size,
            ] = turned.reshape(size // BS, BS, size)


def choose(partner, rows, mirror, mask, block, columns):
    keep = mask[pl.ds(block, 1), columns] > 0.5
    return jnp.where(
        keep,
        rows[source_of(block), :, columns].astype(jnp.float32),
        mirror[partner[block], :, columns],
    )


def fill_first_kernel(partner, acquired, rows, filled, mask, mirror):
    spread(acquired, mask)
    turn(partner, rows, mirror)

    def pick(pair, carry):
        blocks = [
            choose(partner, rows, mirror, mask, pair * 2 + i, slice(None)) for i in range(2)
        ]
        row = pl.multiple_of(pair * 16, 16)
        filled[pl.ds(row, 16), :] = jnp.concatenate(blocks, axis=0).astype(jnp.bfloat16)
        return carry

    lax.fori_loop(0, NB // 2, pick, 0, unroll=8)


def fill_first(partner, acquired, rows):
    vmem = pl.BlockSpec(memory_space=pltpu.VMEM)
    return pl.pallas_call(
        fill_first_kernel,
        out_shape=(
            jax.ShapeDtypeStruct((NS, NS), jnp.bfloat16),
            jax.ShapeDtypeStruct((NB, NS), jnp.float32),
        ),
        in_specs=[pl.BlockSpec(memory_space=pltpu.SMEM), vmem, vmem],
        out_specs=(vmem, vmem),
        scratch_shapes=[pltpu.VMEM((NB, BS, NS), jnp.float32)],
        compiler_params=pltpu.CompilerParams(vmem_limit_bytes=16 * 1024 * 1024),
        name="fill_first",
    )(partner, acquired, rows)


def solve_kernel(
    partner,
    place,
    band_counts,
    wavelet,
    mask,
    first,
    rows,
    out,
    mirror,
    factor,
    left,
    base,
):
    band_end = jnp.int32(0)
    group = jnp.int32(0)
    for g in range(NGROUPS):
        band_end = band_end + band_counts[g]
        group = group + (band_end <= place[2]).astype(jnp.int32)
    rescale = 1.0 / math.sqrt(NS)
    wave_re = wavelet[0, group] * rescale
    wave_im = wavelet[1, group] * rescale
    wave = (
        jnp.where(place[1] == 0, wave_re, -wave_im),
        jnp.where(place[1] == 0, wave_im, -wave_re),
    )
    turn(partner, rows, mirror)

    def scale(columns):
        for pair in range(NB // 2):
            row = pair * 16
            real = first[row : row + 16, columns].astype(jnp.float32)
            imag = jnp.concatenate(
                [choose(partner, rows, mirror, mask, pair * 2 + i, columns) for i in range(2)],
                axis=0,
            )
            factor[row : row + 16, columns] = (wave[0] * real - wave[1] * imag).astype(
                jnp.bfloat16
            )
            factor[NS + row : NS + row + 16, columns] = (
                wave[0] * imag + wave[1] * real
            ).astype(jnp.bfloat16)

    def put(slot, row, rows, real, imag, column, columns):
        real_low = real.astype(jnp.bfloat16)
        imag_low = imag.astype(jnp.bfloat16)
        left[slot, pl.ds(row, rows), pl.ds(column, columns)] = real_low
        left[slot, pl.ds(row, rows), pl.ds(NS + column, columns)] = -imag_low
        left[slot, pl.ds(OWN + row, rows), pl.ds(column, columns)] = imag_low
        left[slot, pl.ds(OWN + row, rows), pl.ds(NS + column, columns)] = real_low

    def own(pair, carry):
        reals, imags = [], []
        for i in range(2):
            member = pair * 2 + i
            chip = (member % 16) * 4 + member // 16 + place[0]
            both = first[pl.ds(pl.multiple_of(chip * 16, 16), 16), :].astype(jnp.float32)
            reals.append(jnp.where(place[1] == 0, both[:BS], both[BS:]))
            imags.append(
                choose(partner, rows, mirror, mask, chip * 2 + place[1], slice(None))
            )
        real = jnp.concatenate(reals, axis=0)
        imag = jnp.concatenate(imags, axis=0)
        row = pl.multiple_of(pair * 16, 16)
        base[pl.ds(row, 16), :] = real
        base[pl.ds(OWN + row, 16), :] = imag
        put(0, row, 16, real, imag, 0, NS)
        return carry

    lax.fori_loop(0, GROUP // 2, own, 0, unroll=4)

    width = 256

    def sweep(slot, first_turn, last):
        for tile in range(NS // width):
            columns = slice(tile * width, (tile + 1) * width)
            if first_turn:
                scale(columns)
            product = jnp.dot(
                left[slot], factor[:, columns], preferred_element_type=jnp.float32
            )
            value = base[:, columns] - product
            if last:
                out[:, 0, :, columns] = (
                    value[:OWN].reshape(GROUP, BS, width).astype(jnp.bfloat16)
                )
                out[:, 1, :, columns] = (
                    value[OWN:].reshape(GROUP, BS, width).astype(jnp.bfloat16)
                )
            else:
                put(1 - slot, 0, OWN, value[:OWN], value[OWN:], tile * width, width)

    for turn_index in range(ITERS):
        sweep(turn_index % 2, turn_index == 0, turn_index == ITERS - 1)


def solve(partner, place, band_counts, wavelet, mask, first, rows):
    smem = pl.BlockSpec(memory_space=pltpu.SMEM)
    vmem = pl.BlockSpec(memory_space=pltpu.VMEM)
    return pl.pallas_call(
        solve_kernel,
        out_shape=jax.ShapeDtypeStruct((GROUP, 2, BS, NS), jnp.bfloat16),
        in_specs=[smem, smem, smem, smem, vmem, vmem, vmem],
        out_specs=vmem,
        scratch_shapes=[
            pltpu.VMEM((NB, BS, NS), jnp.float32),
            pltpu.VMEM((2 * NS, NS), jnp.bfloat16),
            pltpu.VMEM((2, 2 * OWN, 2 * NS), jnp.bfloat16),
            pltpu.VMEM((2 * OWN, NS), jnp.float32),
        ],
        compiler_params=pltpu.CompilerParams(vmem_limit_bytes=32 * 1024 * 1024),
        name="solve",
    )(partner, place, band_counts, wavelet, mask, first, rows)


def shards(recorded, acquired, partner, band_counts, wavelet):
    core = lax.axis_index("core")
    z_hi = lax.axis_index("z_hi")
    my_bin = lax.axis_index("z_lo") * 16 + lax.axis_index("x") * 4 + lax.axis_index("y")
    place = jnp.stack([z_hi * 2, core, my_bin]).astype(jnp.int32)
    forward, inverse = dft_tables()
    ordered = forward.reshape(2, 2, 16, NT).transpose(1, 0, 2, 3).reshape(2 * NF, NT)
    outgoing = transform(
        pltpu.with_memory_space_constraint(jnp.asarray(ordered), pltpu.HBM),
        pltpu.with_memory_space_constraint(recorded, pltpu.HBM),
    )
    first = lax.all_to_all(outgoing, ALL_AXES, split_axis=0, concat_axis=0, tiled=True)
    second = lax.ppermute(first, "core", [(0, 1), (1, 0)])
    filled, mask = fill_first(partner, acquired, first)

    estimate = solve(partner, place, band_counts, wavelet, mask, filled, second)

    returned = lax.all_to_all(estimate, BIN_AXES, split_axis=0, concat_axis=0, tiled=True)
    paired = inverse.reshape(2, NF, NT).transpose(1, 0, 2)
    tables = np.stack([paired.reshape(2 * NF, NT), paired[:, ::-1].reshape(2 * NF, NT)])
    return restore(place, returned, jnp.asarray(tables))


def solution(mesh):
    fine = Mesh(mesh.devices.reshape(2, 2, 2, 4, 4), ALL_AXES)
    return jax.shard_map(
        shards,
        mesh=fine,
        in_specs=(P(SHOT_AXES, None, None), P(), P(), P(), P()),
        out_specs=P(SHOT_AXES, None, None),
        check_vma=False,
    )
```

```python
import math

import jax
import jax.numpy as jnp
import ml_dtypes
import numpy as np
from jax import lax
from jax.experimental import pallas as pl
from jax.experimental.pallas import tpu as pltpu
from jax.sharding import Mesh
from jax.sharding import PartitionSpec as P

NS = 1024
NT = 512
NF = 32
FLO = 4
BS = 8
ITERS = 5
NB = NS // BS
NGROUPS = 8
GROUP = 32
OWN = GROUP * BS
ALL_AXES = ("z_hi", "z_lo", "core", "x", "y")
BIN_AXES = ("z_lo", "x", "y")
SHOT_AXES = ("x", "y", "z_hi", "z_lo", "core")


def dft_tables():
    sample_index = np.arange(NT, dtype=np.int32)
    bin_index = FLO + np.arange(NF, dtype=np.int32)
    angles = (bin_index[:, None] * sample_index[None, :] % NT).astype(np.float32) * np.float32(
        2.0 * math.pi / NT
    )
    cycles = np.concatenate([np.cos(angles), -np.sin(angles)], axis=0).astype(np.float32)
    forward = (cycles * np.float32(1.0 / math.sqrt(NT))).astype(ml_dtypes.bfloat16)
    inverse = (cycles * np.float32(math.sqrt(2.0 / NF))).astype(ml_dtypes.bfloat16)
    return (forward, inverse)


def source_of(block):
    return (block % 8) * 16 + block // 8


def transform_kernel(table_from, traces, out, table, held, wide, sems):
    shots = traces.shape[0]
    copies = [pltpu.make_async_copy(traces.at[s], held.at[s], sems.at[s]) for s in range(shots)]
    table_copy = pltpu.make_async_copy(table_from, table, sems.at[shots])
    table_copy.start()
    for copy in copies:
        copy.start()
    table_copy.wait()
    for s in range(shots):
        copies[s].wait()
        wide[s] = lax.dot_general(
            table[...], held[s], (((1,), (1,)), ((), ())), preferred_element_type=jnp.float32
        )
    ordered = jnp.transpose(wide[...], (1, 0, 2)).astype(jnp.bfloat16)
    out[:64] = ordered
    out[64:] = ordered


def transform(table, traces):
    vmem = pl.BlockSpec(memory_space=pltpu.VMEM)
    return pl.pallas_call(
        transform_kernel,
        out_shape=jax.ShapeDtypeStruct((NB, BS, NS), jnp.bfloat16),
        in_specs=[pl.BlockSpec(memory_space=pltpu.HBM)] * 2,
        out_specs=vmem,
        scratch_shapes=[
            pltpu.VMEM((2 * NF, NT), jnp.bfloat16),
            pltpu.VMEM((BS, NS, NT), jnp.bfloat16),
            pltpu.VMEM((BS, 2 * NF, NS), jnp.float32),
            pltpu.SemaphoreType.DMA((BS + 1,)),
        ],
        compiler_params=pltpu.CompilerParams(vmem_limit_bytes=24 * 1024 * 1024),
        name="transform",
    )(table, traces)


def restore_kernel(place, spectra, tables, out, wide, held, sems):
    wide[...] = jnp.transpose(
        spectra[...].astype(jnp.float32).reshape(2 * NF, BS, NS), (1, 0, 2)
    )
    table = tables[place[1]]
    copies = []
    for s in range(BS):
        held[s] = lax.dot_general(
            wide[s].astype(jnp.bfloat16),
            table,
            (((0,), (0,)), ((), ())),
            preferred_element_type=jnp.float32,
        ).astype(jnp.bfloat16)
        copies.append(pltpu.make_async_copy(held.at[s], out.at[s], sems.at[s]))
        copies[-1].start()
    for copy in copies:
        copy.wait()


def restore(place, spectra, tables):
    vmem = pl.BlockSpec(memory_space=pltpu.VMEM)
    return pl.pallas_call(
        restore_kernel,
        out_shape=jax.ShapeDtypeStruct((BS, NS, NT), jnp.bfloat16),
        in_specs=[pl.BlockSpec(memory_space=pltpu.SMEM), vmem, vmem],
        out_specs=pl.BlockSpec(memory_space=pltpu.HBM),
        scratch_shapes=[
            pltpu.VMEM((BS, 2 * NF, NS), jnp.float32),
            pltpu.VMEM((BS, NS, NT), jnp.bfloat16),
            pltpu.SemaphoreType.DMA((BS,)),
        ],
        compiler_params=pltpu.CompilerParams(vmem_limit_bytes=24 * 1024 * 1024),
        name="restore",
    )(place, spectra, tables)


def spread(acquired, mask):
    column_block = lax.broadcasted_iota(jnp.int32, (NB, NS), 1) // BS
    expand = (column_block == lax.broadcasted_iota(jnp.int32, (NB, NS), 0)).astype(jnp.bfloat16)
    mask[...] = jnp.dot(
        acquired[...].astype(jnp.float32).astype(jnp.bfloat16),
        expand,
        preferred_element_type=jnp.float32,
    )


def turn(partner, rows, mirror):
    size = 256
    identity = (
        lax.broadcasted_iota(jnp.int32, (size, size), 0)
        == lax.broadcasted_iota(jnp.int32, (size, size), 1)
    ).astype(jnp.bfloat16)
    for group in range(NS // size):
        taken = jnp.concatenate(
            [
                rows[source_of(partner[group * (size // BS) + i])].astype(jnp.float32)
                for i in range(size // BS)
            ],
            axis=0,
        ).astype(jnp.bfloat16)
        for tile in range(NS // size):
            turned = lax.dot_general(
                identity,
                taken[:, tile * size : (tile + 1) * size],
                (((1,), (1,)), ((), ())),
                preferred_element_type=jnp.float32,
            )
            mirror[
                tile * (size // BS) : (tile + 1) * (size // BS),
                :,
                group * size : (group + 1) * size,
            ] = turned.reshape(size // BS, BS, size)


def choose(partner, rows, mirror, mask, block, columns):
    keep = mask[pl.ds(block, 1), columns] > 0.5
    return jnp.where(
        keep,
        rows[source_of(block), :, columns].astype(jnp.float32),
        mirror[partner[block], :, columns],
    )


def fill_first_kernel(partner, place, acquired, rows, filled, mask, mine, mirror):
    spread(acquired, mask)
    turn(partner, rows, mirror)

    def pick(pair, carry):
        blocks = [
            choose(partner, rows, mirror, mask, pair * 2 + i, slice(None)) for i in range(2)
        ]
        row = pl.multiple_of(pair * 16, 16)
        filled[pl.ds(row, 16), :] = jnp.concatenate(blocks, axis=0).astype(jnp.bfloat16)
        return carry

    lax.fori_loop(0, NB // 2, pick, 0, unroll=8)

    def gather(pair, carry):
        values = []
        for i in range(2):
            member = pair * 2 + i
            chip = (member % 16) * 4 + member // 16 + place[0]
            both = filled[pl.ds(pl.multiple_of(chip * 16, 16), 16), :].astype(jnp.float32)
            values.append(jnp.where(place[1] == 0, both[:BS], both[BS:]))
        mine[pl.ds(pl.multiple_of(pair * 16, 16), 16), :] = jnp.concatenate(values, axis=0)
        return carry

    lax.fori_loop(0, GROUP // 2, gather, 0, unroll=4)


def fill_first(partner, place, acquired, rows):
    vmem = pl.BlockSpec(memory_space=pltpu.VMEM)
    return pl.pallas_call(
        fill_first_kernel,
        out_shape=(
            jax.ShapeDtypeStruct((NS, NS), jnp.bfloat16),
            jax.ShapeDtypeStruct((NB, NS), jnp.float32),
            jax.ShapeDtypeStruct((OWN, NS), jnp.float32),
        ),
        in_specs=[pl.BlockSpec(memory_space=pltpu.SMEM)] * 2 + [vmem, vmem],
        out_specs=(vmem, vmem, vmem),
        scratch_shapes=[pltpu.VMEM((NB, BS, NS), jnp.float32)],
        compiler_params=pltpu.CompilerParams(vmem_limit_bytes=16 * 1024 * 1024),
        name="fill_first",
    )(partner, place, acquired, rows)


def solve_kernel(
    partner,
    place,
    band_counts,
    wavelet,
    mask,
    mine,
    first,
    rows,
    out,
    mirror,
    factor,
    left,
    base,
):
    band_end = jnp.int32(0)
    group = jnp.int32(0)
    for g in range(NGROUPS):
        band_end = band_end + band_counts[g]
        group = group + (band_end <= place[2]).astype(jnp.int32)
    rescale = 1.0 / math.sqrt(NS)
    wave_re = wavelet[0, group] * rescale
    wave_im = wavelet[1, group] * rescale
    wave = (
        jnp.where(place[1] == 0, wave_re, -wave_im),
        jnp.where(place[1] == 0, wave_im, -wave_re),
    )
    turn(partner, rows, mirror)

    def scale(columns):
        for pair in range(NB // 2):
            row = pair * 16
            real = first[row : row + 16, columns].astype(jnp.float32)
            imag = jnp.concatenate(
                [choose(partner, rows, mirror, mask, pair * 2 + i, columns) for i in range(2)],
                axis=0,
            )
            factor[row : row + 16, columns] = (wave[0] * real - wave[1] * imag).astype(
                jnp.bfloat16
            )
            factor[NS + row : NS + row + 16, columns] = (
                wave[0] * imag + wave[1] * real
            ).astype(jnp.bfloat16)

    def put(slot, row, rows, real, imag, column, columns):
        real_low = real.astype(jnp.bfloat16)
        imag_low = imag.astype(jnp.bfloat16)
        left[slot, pl.ds(row, rows), pl.ds(column, columns)] = real_low
        left[slot, pl.ds(row, rows), pl.ds(NS + column, columns)] = -imag_low
        left[slot, pl.ds(OWN + row, rows), pl.ds(column, columns)] = imag_low
        left[slot, pl.ds(OWN + row, rows), pl.ds(NS + column, columns)] = real_low

    def own(pair, carry):
        imags = []
        for i in range(2):
            member = pair * 2 + i
            chip = (member % 16) * 4 + member // 16 + place[0]
            imags.append(
                choose(partner, rows, mirror, mask, chip * 2 + place[1], slice(None))
            )
        row = pl.multiple_of(pair * 16, 16)
        real = mine[pl.ds(row, 16), :]
        imag = jnp.concatenate(imags, axis=0)
        base[pl.ds(row, 16), :] = imag
        put(0, row, 16, real, imag, 0, NS)
        return carry

    lax.fori_loop(0, GROUP // 2, own, 0, unroll=4)

    width = 256

    def sweep(slot, first_turn, last):
        for tile in range(NS // width):
            columns = slice(tile * width, (tile + 1) * width)
            if first_turn:
                scale(columns)
            product = jnp.dot(
                left[slot], factor[:, columns], preferred_element_type=jnp.float32
            )
            real = mine[:, columns] - product[:OWN]
            imag = base[:, columns] - product[OWN:]
            if last:
                out[:, 0, :, columns] = (
                    real.reshape(GROUP, BS, width).astype(jnp.bfloat16)
                )
                out[:, 1, :, columns] = (
                    imag.reshape(GROUP, BS, width).astype(jnp.bfloat16)
                )
            else:
                put(1 - slot, 0, OWN, real, imag, tile * width, width)

    for turn_index in range(ITERS):
        sweep(turn_index % 2, turn_index == 0, turn_index == ITERS - 1)


def solve(partner, place, band_counts, wavelet, mask, mine, first, rows):
    smem = pl.BlockSpec(memory_space=pltpu.SMEM)
    vmem = pl.BlockSpec(memory_space=pltpu.VMEM)
    return pl.pallas_call(
        solve_kernel,
        out_shape=jax.ShapeDtypeStruct((GROUP, 2, BS, NS), jnp.bfloat16),
        in_specs=[smem, smem, smem, smem, vmem, vmem, vmem, vmem],
        out_specs=vmem,
        scratch_shapes=[
            pltpu.VMEM((NB, BS, NS), jnp.float32),
            pltpu.VMEM((2 * NS, NS), jnp.bfloat16),
            pltpu.VMEM((2, 2 * OWN, 2 * NS), jnp.bfloat16),
            pltpu.VMEM((OWN, NS), jnp.float32),
        ],
        compiler_params=pltpu.CompilerParams(vmem_limit_bytes=32 * 1024 * 1024),
        name="solve",
    )(partner, place, band_counts, wavelet, mask, mine, first, rows)


def shards(recorded, acquired, partner, band_counts, wavelet):
    core = lax.axis_index("core")
    z_hi = lax.axis_index("z_hi")
    my_bin = lax.axis_index("z_lo") * 16 + lax.axis_index("x") * 4 + lax.axis_index("y")
    place = jnp.stack([z_hi * 2, core, my_bin]).astype(jnp.int32)
    forward, inverse = dft_tables()
    ordered = forward.reshape(2, 2, 16, NT).transpose(1, 0, 2, 3).reshape(2 * NF, NT)
    outgoing = transform(
        pltpu.with_memory_space_constraint(jnp.asarray(ordered), pltpu.HBM),
        pltpu.with_memory_space_constraint(recorded, pltpu.HBM),
    )
    first = lax.all_to_all(outgoing, ALL_AXES, split_axis=0, concat_axis=0, tiled=True)
    second = lax.ppermute(first, "core", [(0, 1), (1, 0)])
    filled, mask, mine = fill_first(partner, place, acquired, first)

    estimate = solve(partner, place, band_counts, wavelet, mask, mine, filled, second)

    returned = lax.all_to_all(estimate, BIN_AXES, split_axis=0, concat_axis=0, tiled=True)
    paired = inverse.reshape(2, NF, NT).transpose(1, 0, 2)
    tables = np.stack([paired.reshape(2 * NF, NT), paired[:, ::-1].reshape(2 * NF, NT)])
    return restore(place, returned, jnp.asarray(tables))


def solution(mesh):
    fine = Mesh(mesh.devices.reshape(2, 2, 2, 4, 4), ALL_AXES)
    return jax.shard_map(
        shards,
        mesh=fine,
        in_specs=(P(SHOT_AXES, None, None), P(), P(), P(), P()),
        out_specs=P(SHOT_AXES, None, None),
        check_vma=False,
    )
```
